256 devices in a mesh: dp: 32 (over y, x, core), mp: 8 (over z).
Axes of the slice: x: 4, y: 4, z: 8, core: 2. Of those that a mesh axis runs over, the one named last changes fastest.
Arguments:
- gradients: bfloat16 [32, 32, 2048, 256], P('dp', None, 'mp'), may hold values from -0.21875 to 0.21875
- owners: int32 [32], replicated, may hold values from 0 to 31, as said below
- left_stat: float32 [64, 2048, 256], P('dp', 'mp'), as said below
- left_basis: float32 [64, 2048, 256], P('dp', 'mp'), as said below
- right_stat: float32 [64, 256, 256], P('dp'), as said below
- right_basis: float32 [64, 256, 256], P('dp'), as said below
- momentum: float32 [64, 2048, 256], P('dp', 'mp'), may hold values from -1.2 to 1.2
- second_moment: float32 [64, 2048, 256], P('dp', 'mp'), may hold values from 0.01 to 0.1
Outputs:
- new_left_stat: float32 [64, 2048, 256], P('dp', 'mp')
- new_left_basis: float32 [64, 2048, 256], P('dp', 'mp')
- new_right_stat: float32 [64, 256, 256], P('dp')
- new_right_basis: float32 [64, 256, 256], P('dp')
- new_momentum: float32 [64, 2048, 256], P('dp', 'mp')
- new_second_moment: float32 [64, 2048, 256], P('dp', 'mp')
- update: float32 [64, 2048, 256], P('dp', 'mp')
The draws below stay inside these ranges and needn't reach their ends.
Inputs may be any that keep to these rules, and one draw needn't show every extreme that they name: `owners`: a quarter of the dp indices own exactly 2 units each, half of the dp indices own half as many each, and the remaining quarter own none; which indices and which units are drawn. `left_stat`: each block is symmetric positive definite. `right_stat`: symmetric positive definite. `left_basis`: each block is nonsingular. `right_basis`: nonsingular.
All inputs are finite; a program needn't handle non-finite values.
Results may differ from the reference program's by a relative error of at most 0.00065.
Values may be sent and summed in bfloat16 or wider, within the bound.
A program may use at most 128 MiB of HBM per device.

```python
import math
import jax
import jax.numpy as jnp
from jax import lax

D = 2048
BLK = 256
UNITS = 32
OWN_MAX = 2
SLOTS = 64
N_DP = 32


def rough_normal(key, shape):
    return jax.random.normal(key, shape, jnp.float32)


def symmetric_blocks(key, count, size):
    key_off, key_diag = jax.random.split(key)
    raw = rough_normal(key_off, (count, size, size))
    spread = (raw + jnp.swapaxes(raw, 1, 2)) * (1.0 / math.sqrt(2.0 * size))
    diagonal = jnp.exp(jax.random.uniform(key_diag, (count, size), jnp.float32, math.log(4.0), math.log(8.0)))
    identity = jnp.eye(size, dtype=jnp.float32)
    return spread * (1.0 - identity) + identity * diagonal[:, :, None]


def near_identity(key, count, size):
    raw = rough_normal(key, (count, size, size))
    identity = jnp.eye(size, dtype=jnp.float32)
    return identity[None, :, :] + raw * (0.3 / math.sqrt(size))


def draw_left_stat(key, part):
    return symmetric_blocks(jax.random.fold_in(key, 11), SLOTS * (D // BLK), BLK).reshape(SLOTS, D, BLK)


def draw_right_stat(key, part):
    return symmetric_blocks(jax.random.fold_in(key, 12), SLOTS, BLK)


def draw_left_basis(key, part):
    return near_identity(jax.random.fold_in(key, 13), SLOTS * (D // BLK), BLK).reshape(SLOTS, D, BLK)


def draw_right_basis(key, part):
    return near_identity(jax.random.fold_in(key, 14), SLOTS, BLK)


def draw_owners(key, part):
    key_rank, key_unit = jax.random.split(jax.random.fold_in(key, 15))
    device_order = jax.random.permutation(key_rank, N_DP).astype(jnp.int32)
    position_list = jnp.arange(UNITS, dtype=jnp.int32)
    heavy_units = N_DP // 4 * OWN_MAX
    rank_position = jnp.where(position_list < heavy_units, position_list // OWN_MAX, N_DP // 4 + (position_list - heavy_units) // (OWN_MAX // 2))
    sequence = device_order[rank_position]
    shuffle = jax.random.permutation(key_unit, UNITS)
    return jnp.zeros((UNITS,), jnp.int32).at[shuffle].set(sequence)


def steps_of(rng, extent, cuts, low, top_value):
    factor_of, own = 1.0, jax.random.fold_in(rng, 6)
    for axis_at, shards_of in cuts:
        heights = jnp.exp(jax.random.uniform(jax.random.fold_in(own, axis_at), (shards_of,), jnp.float32, low / len(cuts), top_value / len(cuts)))
        factor_of = factor_of * jnp.repeat(heights, extent[axis_at] // shards_of).reshape([-1 if axis == axis_at else 1 for axis in range(len(extent))])
    return factor_of


def normal_values(own_key, dims, deviation, reach, cuts=(), held_as=jnp.bfloat16):
    gain = steps_of(own_key, dims, cuts, -0.22, 0.18) if cuts else 1.0
    values = jax.random.normal(own_key, dims, jnp.float32) * deviation * gain
    return jnp.minimum(jnp.maximum(values, -reach), reach).astype(held_as)


def setup_inputs(seed: int = 0) -> dict:
    streams_of = jax.random.split(jax.random.key(seed), 9)
    gradients = normal_values(streams_of[0], (N_DP, UNITS, D, BLK), (25 * N_DP) ** -0.5, 0.21875, ((0, 32), (2, 8)))
    owners = draw_owners(jax.random.fold_in(streams_of[8], 71), 0)
    left_stat = draw_left_stat(jax.random.fold_in(streams_of[8], 71), 0)
    left_basis = draw_left_basis(jax.random.fold_in(streams_of[8], 71), 0)
    right_stat = draw_right_stat(jax.random.fold_in(streams_of[8], 71), 0)
    right_basis = draw_right_basis(jax.random.fold_in(streams_of[8], 71), 0)
    momentum = normal_values(streams_of[6], (SLOTS, D, BLK), 0.2, 1.2, ((0, 32), (1, 8)), jnp.float32)
    second_moment = jnp.clip(jnp.exp(math.log(0.1) - 2.3025851 * jax.random.uniform(streams_of[7], (SLOTS, D, BLK), jnp.float32) ** steps_of(streams_of[7], (SLOTS, D, BLK), ((0, 32), (1, 8)), -0.2, 0.2)), 0.01, 0.1)
    return dict(gradients=gradients, owners=owners, left_stat=left_stat, left_basis=left_basis, right_stat=right_stat, right_basis=right_basis, momentum=momentum, second_moment=second_moment)


decay_first = 0.9
decay_second = 0.95
epsilon = 1e-08
highest = lax.Precision.HIGHEST

def slot_table(owners, per_device, slot_total):
    unit_count = owners.shape[0]
    positions = jnp.arange(unit_count, dtype=jnp.int32)
    earlier = (owners[:, None] == owners[None, :]) & (positions[None, :] < positions[:, None])
    rank_before = lax.optimization_barrier(jnp.sum(earlier.astype(jnp.int32), axis=1)).astype(jnp.int32)
    slot_index = owners * per_device + rank_before
    targets = jnp.arange(slot_total, dtype=jnp.int32)
    matches = (slot_index[None, :] == targets[:, None]).astype(jnp.int32)
    unit_of = lax.optimization_barrier(jnp.sum(matches * positions[None, :], axis=1)).astype(jnp.int32)
    filled = lax.optimization_barrier(jnp.sum(matches, axis=1)).astype(jnp.int32)
    return (unit_of, filled)

def orthonormal_rows(rows_in):
    gram_matrix = jnp.einsum('...ik,...jk->...ij', rows_in, rows_in, precision=highest)
    factor = jnp.linalg.cholesky(gram_matrix)
    return jax.scipy.linalg.solve_triangular(factor, rows_in, lower=True)

def one_slot(items):
    gradient, left_stat, left_basis, right_stat, right_basis, momentum, second_moment = items
    block_shape = (D // BLK, BLK, BLK)
    grad_blocks = gradient.reshape(block_shape).astype(jnp.float32)
    left_blocks = left_stat.reshape(block_shape)
    basis_blocks = left_basis.reshape(block_shape)
    moment_blocks = momentum.reshape(block_shape)
    square_blocks = second_moment.reshape(block_shape)
    left_term = jnp.einsum('rik,rjk->rij', grad_blocks, grad_blocks, precision=highest)
    right_term = jnp.einsum('rki,rkj->ij', grad_blocks, grad_blocks, precision=highest)
    new_left = decay_second * left_blocks + (1.0 - decay_second) * left_term
    new_right = decay_second * right_stat + (1.0 - decay_second) * right_term
    new_moment = decay_first * moment_blocks + (1.0 - decay_first) * grad_blocks

    def rotate(values):
        inner = jnp.einsum('rij,rjk->rik', basis_blocks, values, precision=highest)
        return jnp.einsum('rik,lk->ril', inner, right_basis, precision=highest)
    rotated_gradient = rotate(grad_blocks)
    rotated_momentum = rotate(new_moment)
    new_square = decay_second * square_blocks + (1.0 - decay_second) * rotated_gradient * rotated_gradient
    normed = rotated_momentum / (jnp.sqrt(new_square) + epsilon)
    restored = jnp.einsum('rji,rjk->rik', basis_blocks, normed, precision=highest)
    update = jnp.einsum('rik,kl->ril', restored, right_basis, precision=highest)
    new_left_basis = orthonormal_rows(jnp.einsum('rij,rjk->rik', basis_blocks, new_left, precision=highest))
    new_right_basis = orthonormal_rows(jnp.dot(right_basis, new_right, precision=highest))
    return (new_left.reshape(D, BLK), new_left_basis.reshape(D, BLK), new_right, new_right_basis, new_moment.reshape(D, BLK), new_square.reshape(D, BLK), update.reshape(D, BLK))

def reference(gradients, owners, left_stat, left_basis, right_stat, right_basis, momentum, second_moment):

    def add_part(carry, part):
        return (carry + part.astype(jnp.float32), None)
    summed, _ = lax.scan(add_part, jnp.zeros((UNITS, D, BLK), jnp.float32), gradients)
    summed = summed.astype(jnp.bfloat16)
    unit_of, filled = slot_table(owners, OWN_MAX, SLOTS)
    per_slot = jnp.take(summed, unit_of, axis=0) * filled.astype(jnp.bfloat16)[:, None, None]
    results = lax.map(one_slot, (per_slot, left_stat, left_basis, right_stat, right_basis, momentum, second_moment))
    return (results[0], results[1], results[2], results[3], results[4], results[5], results[6])
```

```python
import jax
import jax.numpy as jnp
from jax import lax
from jax.experimental import pallas as pl
from jax.experimental.pallas import tpu as pltpu
from jax.sharding import PartitionSpec as P

HI = lax.Precision.HIGHEST
F32 = jnp.float32
MESH = pl.DeviceIdType.MESH
NB = 64
N = 256


def mm(a, b):
    return lax.dot_general(a, b, (((1,), (0,)), ((), ())), precision=HI, preferred_element_type=F32)


def mm_nt(a, b):
    return lax.dot_general(a, b, (((1,), (1,)), ((), ())), precision=HI, preferred_element_type=F32)


def mm_tn(a, b):
    return lax.dot_general(a, b, (((0,), (0,)), ((), ())), precision=HI, preferred_element_type=F32)


def row_of(x, s):
    return jnp.broadcast_to(x[s : s + 1, :], x.shape)


def factor_blocks(blocks):
    count = len(blocks)
    tiles = NB // 8
    rows = [[b[8 * r : 8 * r + 8, :] for r in range(tiles)] for b in blocks]
    sub = lax.broadcasted_iota(jnp.int32, (8, 128), 0)
    done = [[] for _ in range(count)]
    for q in range(tiles):
        j0 = 8 * q
        for m in range(count):
            cols = [
                [jnp.broadcast_to(rows[m][r][:, j0 + s : j0 + s + 1], (8, 128)) for r in range(q, tiles)]
                for s in range(8)
            ]
            scale = None
            top = rows[m][q]
            rest = rows[m][q + 1 :]
            for s in range(8):
                d = row_of(cols[s][0], s)
                inv = 1.0 / d
                root = lax.rsqrt(d)
                scale = root if scale is None else jnp.where(sub >= s, root, scale)
                mult = [c * inv for c in cols[s]]
                for s2 in range(s + 1, 8):
                    f = row_of(cols[s][0], s2)
                    cols[s2] = [c - mu * f for c, mu in zip(cols[s2], mult)]
                u = row_of(top, s)
                if s < 7:
                    top = top - jnp.where(sub > s, mult[0], 0.0) * u
                rest = [x - mu * u for x, mu in zip(rest, mult[1:])]
            done[m].append(top * scale)
            rows[m][q + 1 :] = rest
    return [jnp.concatenate(d, axis=0) for d in done]


def orth_all(y_refs, s_ref, out_refs):
    count = len(y_refs)
    r_i = lax.broadcasted_iota(jnp.int32, (NB, NB), 0)
    c_i = lax.broadcasted_iota(jnp.int32, (NB, NB), 1)
    eye = (r_i == c_i).astype(F32)
    for m in range(count):
        y = y_refs[m][...]
        s_ref[m] = mm_nt(y, y)
    for k in range(N // NB):
        k0 = k * NB
        blocks = [
            jnp.concatenate([s_ref[m, k0 : k0 + NB, k0 : k0 + NB], eye], axis=1)
            for m in range(count)
        ]
        factors = factor_blocks(blocks)
        for m in range(count):
            inv = factors[m][:, NB : 2 * NB]
            w_y = mm(inv, y_refs[m][k0 : k0 + NB, :])
            out_refs[m][k0 : k0 + NB, :] = w_y
            t0 = k0 + NB
            if t0 < N:
                c0 = t0 // 128 * 128
                w_s = mm(inv, s_ref[m, k0 : k0 + NB, c0:])
                lead = w_s[:, t0 - c0 :]
                s_ref[m, t0:, c0:] = s_ref[m, t0:, c0:] - mm_tn(lead, w_s)
                y_refs[m][t0:, :] = y_refs[m][t0:, :] - mm_tn(lead, w_y)


def comm_kernel(g_ref, owners_ref, grad_ref, right_ref,
                ra, rb, sa, sb, ra2, rb2, aga, agb, pbuf, prec, part, rz, res,
                s1a, r1a, s1b, r1b, s2a, r2a, s2b, r2b, s3a, r3a, s3b, r3b,
                s4a, r4a, s4b, r4b, sp, rp, sza, rza, szb, rzb, local_sem):
    me = lax.axis_index("dp")
    z = lax.axis_index("mp")
    c = me % 2
    x = (me // 2) % 4
    y = me // 8
    row_id = x * 2 + c
    col_id = y * 2 + c
    top, low = pl.ds(0, 128), pl.ds(128, 128)

    def dev(yy, xx, cc):
        return {"dp": yy * 8 + xx * 2 + cc}

    def remote(src, dst, s, r, device):
        return pltpu.make_async_remote_copy(
            src_ref=src, dst_ref=dst, send_sem=s, recv_sem=r, device_id=device, device_id_type=MESH
        )

    own_a = pltpu.make_async_copy(g_ref.at[:, x, c, top, :], ra.at[7], local_sem.at[0])
    own_b = pltpu.make_async_copy(g_ref.at[y, :, c, low, :], rb.at[7], local_sem.at[1])
    own_a.start()
    own_b.start()

    barrier = pltpu.get_barrier_semaphore()
    for j in range(1, 8):
        r = (row_id + j) % 8
        q = (col_id + j) % 8
        pl.semaphore_signal(barrier, inc=1, device_id=dev(y, r // 2, r % 2), device_id_type=MESH)
        pl.semaphore_signal(barrier, inc=1, device_id=dev(q // 2, x, q % 2), device_id_type=MESH)
        pl.semaphore_signal(barrier, inc=1, device_id={"mp": (z + j) % 8}, device_id_type=MESH)
    pl.semaphore_wait(barrier, 21)

    first_a, first_b = [], []
    for j in range(1, 8):
        r = (row_id + j) % 8
        q = (col_id + j) % 8
        first_a.append(remote(g_ref.at[:, r // 2, r % 2, top, :], ra.at[j - 1],
                              s1a.at[j - 1], r1a.at[j - 1], dev(y, r // 2, r % 2)))
        first_b.append(remote(g_ref.at[q // 2, :, q % 2, low, :], rb.at[j - 1],
                              s1b.at[j - 1], r1b.at[j - 1], dev(q // 2, x, q % 2)))
    for a, b in zip(first_a, first_b):
        a.start()
        b.start()

    def slots_of(owner):
        seen = jnp.int32(0)
        unit = [jnp.int32(0), jnp.int32(0)]
        found = [jnp.int32(0), jnp.int32(0)]
        for u in range(32):
            hit = jnp.where(owners_ref[u] == owner, 1, 0)
            for t in range(2):
                now = jnp.where(seen == t, hit, 0)
                unit[t] = unit[t] + now * u
                found[t] = found[t] + now
            seen = seen + hit
        return unit, found

    mine, mine_found = slots_of(me)
    other, other_found = slots_of(me + 1 - 2 * c)

    own_a.wait()
    own_b.wait()
    for a, b in zip(first_a, first_b):
        a.wait_recv()
        b.wait_recv()

    second_a, second_b = [], []

    def total(buf, k):
        acc = buf[7, k].astype(F32)
        for s in range(7):
            acc = acc + buf[s, k].astype(F32)
        return acc

    for j in range(1, 4):
        yk = (y + j) % 4
        xk = (x + j) % 4
        sa[j - 1] = total(ra, yk)
        a = remote(sa.at[j - 1], ra2.at[j - 1], s2a.at[j - 1], r2a.at[j - 1], dev(yk, x, c))
        a.start()
        sb[j - 1] = total(rb, xk)
        b = remote(sb.at[j - 1], rb2.at[j - 1], s2b.at[j - 1], r2b.at[j - 1], dev(y, xk, c))
        b.start()
        second_a.append(a)
        second_b.append(b)
    keep_a = total(ra, y)
    keep_b = total(rb, x)
    for a in second_a:
        a.wait_recv()
    for s in range(3):
        keep_a = keep_a + ra2[s]
    aga[y, x] = keep_a.astype(jnp.bfloat16)
    third_a, third_b = [], []
    for j in range(1, 4):
        a = remote(aga.at[y, x], aga.at[y, x], s3a.at[j - 1], r3a.at[j - 1], dev((y + j) % 4, x, c))
        a.start()
        third_a.append(a)
    for b in second_b:
        b.wait_recv()
    for s in range(3):
        keep_b = keep_b + rb2[s]
    agb[y, x] = keep_b.astype(jnp.bfloat16)
    for j in range(1, 4):
        b = remote(agb.at[y, x], agb.at[y, x], s3b.at[j - 1], r3b.at[j - 1], dev(y, (x + j) % 4, c))
        b.start()
        third_b.append(b)
    for j in range(1, 4):
        remote(aga.at[y, x], aga.at[(y + 4 - j) % 4, x], s3a.at[j - 1], r3a.at[j - 1],
               dev((y + j) % 4, x, c)).wait_recv()
    fourth_a, fourth_b = [], []
    for j in range(1, 4):
        a = remote(aga.at[:, x], aga.at[:, x], s4a.at[j - 1], r4a.at[j - 1], dev(y, (x + j) % 4, c))
        a.start()
        fourth_a.append(a)
    for j in range(1, 4):
        remote(agb.at[y, x], agb.at[y, (x + 4 - j) % 4], s3b.at[j - 1], r3b.at[j - 1],
               dev(y, (x + j) % 4, c)).wait_recv()
    for j in range(1, 4):
        b = remote(agb.at[y], agb.at[y], s4b.at[j - 1], r4b.at[j - 1], dev((y + j) % 4, x, c))
        b.start()
        fourth_b.append(b)
    for j in range(1, 4):
        remote(aga.at[:, x], aga.at[:, (x + 4 - j) % 4], s4a.at[j - 1], r4a.at[j - 1],
               dev(y, (x + j) % 4, c)).wait_recv()
        remote(agb.at[y], agb.at[(y + 4 - j) % 4], s4b.at[j - 1], r4b.at[j - 1],
               dev((y + j) % 4, x, c)).wait_recv()

    def pick(buf, unit, flag):
        return buf[unit // 8, (unit // 2) % 4].astype(F32) * flag

    def flag_of(unit, found):
        return jnp.where(unit % 2 == c, found, 0).astype(F32)

    for t in range(2):
        flag = flag_of(other[t], other_found[t])
        pbuf[t, 0:128, :] = pick(aga, other[t], flag).astype(jnp.bfloat16)
        pbuf[t, 128:256, :] = pick(agb, other[t], flag).astype(jnp.bfloat16)
    pair = remote(pbuf, prec, sp, rp, dev(y, x, 1 - c))
    pair.start()
    kept = []
    for t in range(2):
        flag = flag_of(mine[t], mine_found[t])
        kept.append((pick(aga, mine[t], flag), pick(agb, mine[t], flag)))
    pair.wait_recv()
    for t in range(2):
        grad = jnp.concatenate(
            [kept[t][0] + prec[t, 0:128, :].astype(F32), kept[t][1] + prec[t, 128:256, :].astype(F32)], axis=0
        ).astype(jnp.bfloat16)
        grad_ref[t] = grad
        g0, g1 = grad[:, 0:128], grad[:, 128:256]
        for i, (p, q) in enumerate(((g0, g0), (g0, g1), (g1, g1))):
            part[3 * t + i] = lax.dot_general(p, q, (((0,), (0,)), ((), ())), preferred_element_type=F32)

    zsend = []
    for j in range(1, 8):
        zk = (z + j) % 8
        a = remote(part.at[:, pl.ds(pl.multiple_of(zk * 16, 16), 16), :], rz.at[j - 1],
                   sza.at[j - 1], rza.at[j - 1], {"mp": zk})
        a.start()
        zsend.append(a)
    acc = part[:, pl.ds(pl.multiple_of(z * 16, 16), 16), :]
    for j in range(1, 8):
        zsend[j - 1].wait_recv()
        acc = acc + rz[j - 1]
    res[z] = acc
    zgather = []
    for j in range(1, 8):
        a = remote(res.at[z], res.at[z], szb.at[j - 1], rzb.at[j - 1], {"mp": (z + j) % 8})
        a.start()
        zgather.append(a)
    for j in range(1, 8):
        remote(res.at[z], res.at[(z + 8 - j) % 8], szb.at[j - 1], rzb.at[j - 1],
               {"mp": (z + j) % 8}).wait_recv()
    for k in range(8):
        right_ref[:, 16 * k : 16 * k + 16, :] = res[k]
    for copy in (first_a + first_b + second_a + second_b + third_a + third_b + fourth_a + fourth_b
                 + [pair] + zsend + zgather):
        copy.wait_send()


def exchange(gradients, owners):
    bf, f32 = jnp.bfloat16, F32
    dma = pltpu.SemaphoreType.DMA
    return pl.pallas_call(
        comm_kernel,
        out_shape=(
            jax.ShapeDtypeStruct((2, 256, 256), bf),
            jax.ShapeDtypeStruct((6, 128, 128), f32),
        ),
        in_specs=[
            pl.BlockSpec(memory_space=pl.ANY),
            pl.BlockSpec(memory_space=pltpu.SMEM),
        ],
        out_specs=(
            pl.BlockSpec(memory_space=pltpu.VMEM),
            pl.BlockSpec(memory_space=pltpu.VMEM),
        ),
        scratch_shapes=[
            pltpu.VMEM((8, 4, 128, 256), bf), pltpu.VMEM((8, 4, 128, 256), bf),
            pltpu.VMEM((3, 128, 256), f32), pltpu.VMEM((3, 128, 256), f32),
            pltpu.VMEM((3, 128, 256), f32), pltpu.VMEM((3, 128, 256), f32),
            pltpu.VMEM((4, 4, 128, 256), bf), pltpu.VMEM((4, 4, 128, 256), bf),
            pltpu.VMEM((2, 256, 256), bf), pltpu.VMEM((2, 256, 256), bf),
            pltpu.VMEM((6, 128, 128), f32), pltpu.VMEM((7, 6, 16, 128), f32),
            pltpu.VMEM((8, 6, 16, 128), f32),
            dma((7,)), dma((7,)), dma((7,)), dma((7,)),
            dma((3,)), dma((3,)), dma((3,)), dma((3,)),
            dma((3,)), dma((3,)), dma((3,)), dma((3,)),
            dma((3,)), dma((3,)), dma((3,)), dma((3,)),
            dma, dma, dma((7,)), dma((7,)), dma((7,)), dma((7,)), dma((2,)),
        ],
        compiler_params=pltpu.CompilerParams(collective_id=0, has_side_effects=True),
        name="exchange",
    )(gradients.reshape(4, 4, 2, 256, 256), owners)


def local_kernel(grad_ref, right_ref, l_ref, p_ref, r_ref, q_ref, m_ref, v_ref,
                 nl_ref, nlb_ref, nr_ref, nrb_ref, nm_ref, nv_ref, up_ref, work, s_ref):
    for t in range(2):
        g = grad_ref[t]
        new_left = 0.95 * l_ref[t] + 0.05 * lax.dot_general(
            g, g, (((1,), (1,)), ((), ())), preferred_element_type=F32
        )
        nl_ref[t] = new_left
        work[t] = mm(p_ref[t], new_left)
        s01 = right_ref[3 * t + 1]
        right_sum = jnp.concatenate(
            [
                jnp.concatenate([right_ref[3 * t], s01], axis=1),
                jnp.concatenate([s01.T, right_ref[3 * t + 2]], axis=1),
            ],
            axis=0,
        )
        new_right = 0.95 * r_ref[t] + 0.05 * right_sum
        nr_ref[t] = new_right
        work[2 + t] = mm(q_ref[t], new_right)
    for t in range(2):
        g = grad_ref[t].astype(F32)
        new_m = 0.9 * m_ref[t] + 0.1 * g
        nm_ref[t] = new_m
        p, q = p_ref[t], q_ref[t]
        rot_g = mm_nt(mm(p, g), q)
        rot_m = mm_nt(mm(p, new_m), q)
        new_v = 0.95 * v_ref[t] + 0.05 * rot_g * rot_g
        nv_ref[t] = new_v
        normed = rot_m / (jnp.sqrt(new_v) + 1e-8)
        up_ref[t] = mm(mm_tn(p, normed), q)
    outs = [nlb_ref.at[0], nlb_ref.at[1], nrb_ref.at[0], nrb_ref.at[1]]
    orth_all([work.at[m] for m in range(4)], s_ref, outs)


def local_step(*args):
    shape = jax.ShapeDtypeStruct((2, N, N), F32)
    vmem = pl.BlockSpec(memory_space=pltpu.VMEM)
    return pl.pallas_call(
        local_kernel,
        out_shape=(shape,) * 7,
        in_specs=[vmem] * 8,
        out_specs=(vmem,) * 7,
        scratch_shapes=[pltpu.VMEM((4, N, N), F32), pltpu.VMEM((4, N, N), F32)],
        name="local_step",
    )(*args)


def on_device(
    gradients, owners, left_stat, left_basis, right_stat, right_basis, momentum, second_moment
):
    gradient, right_sum = exchange(gradients[0], owners)
    return local_step(
        gradient, right_sum, left_stat, left_basis, right_stat, right_basis, momentum, second_moment
    )


def solution(mesh):
    big, small = P("dp", "mp", None), P("dp", None, None)
    return jax.shard_map(
        on_device,
        mesh=mesh,
        in_specs=(P("dp", None, "mp", None), P(), big, big, small, small, big, big),
        out_specs=(big, big, small, small, big, big, big),
        check_vma=False,
    )
```

```python
import functools
import jax
import jax.numpy as jnp
from jax import lax
from jax.experimental import pallas as pl
from jax.experimental.pallas import tpu as pltpu
from jax.sharding import PartitionSpec as P

HI = lax.Precision.HIGHEST
F32 = jnp.float32
MESH = pl.DeviceIdType.MESH
NB = 64
N = 256
FILL_EVERY = 1
FILL_AT = 0


def mm(a, b):
    return lax.dot_general(a, b, (((1,), (0,)), ((), ())), precision=HI, preferred_element_type=F32)


def mm_nt(a, b):
    return lax.dot_general(a, b, (((1,), (1,)), ((), ())), precision=HI, preferred_element_type=F32)


def mm_tn(a, b):
    return lax.dot_general(a, b, (((0,), (0,)), ((), ())), precision=HI, preferred_element_type=F32)


def row_of(x, s):
    return jnp.broadcast_to(x[s : s + 1, :], x.shape)


def factor_blocks(blocks, fillers):
    count = len(blocks)
    tiles = NB // 8
    rows = [[b[8 * r : 8 * r + 8, :] for r in range(tiles)] for b in blocks]
    sub = lax.broadcasted_iota(jnp.int32, (8, 128), 0)
    done = [[] for _ in range(count)]
    for q in range(tiles):
        j0 = 8 * q
        if fillers and q % FILL_EVERY == FILL_AT:
            fillers.pop(0)()
        for m in range(count):
            cols = [
                [jnp.broadcast_to(rows[m][r][:, j0 + s : j0 + s + 1], (8, 2 * NB)) for r in range(q, tiles)]
                for s in range(8)
            ]
            scale = None
            top = rows[m][q]
            rest = rows[m][q + 1 :]
            for s in range(8):
                d = row_of(cols[s][0], s)
                inv = 1.0 / d
                root = lax.rsqrt(d)
                scale = root if scale is None else jnp.where(sub >= s, root, scale)
                mult = [c * inv for c in cols[s]]
                for s2 in range(s + 1, 8):
                    f = row_of(cols[s][0], s2)
                    cols[s2] = [c - mu * f for c, mu in zip(cols[s2], mult)]
                u = row_of(top, s)
                if s < 7:
                    top = top - jnp.where(sub > s, mult[0], 0.0) * u
                rest = [x - mu * u for x, mu in zip(rest, mult[1:])]
            done[m].append(top * scale)
            rows[m][q + 1 :] = rest
    return [jnp.concatenate(d, axis=0) for d in done]


def orth_all(y_refs, s_ref, out_refs, fillers):
    count = len(y_refs)
    r_i = lax.broadcasted_iota(jnp.int32, (NB, NB), 0)
    c_i = lax.broadcasted_iota(jnp.int32, (NB, NB), 1)
    eye = (r_i == c_i).astype(F32)
    for m in range(count):
        y = y_refs[m][...]
        s_ref[m] = mm_nt(y, y)
    for k in range(N // NB):
        k0 = k * NB
        blocks = [
            jnp.concatenate([s_ref[m, k0 : k0 + NB, k0 : k0 + NB], eye], axis=1)
            for m in range(count)
        ]
        factors = factor_blocks(blocks, fillers)
        for m in range(count):
            inv = factors[m][:, NB : 2 * NB]
            w_y = mm(inv, y_refs[m][k0 : k0 + NB, :])
            out_refs[m][k0 : k0 + NB, :] = w_y
            t0 = k0 + NB
            if t0 < N:
                c0 = t0 // 128 * 128
                w_s = mm(inv, s_ref[m, k0 : k0 + NB, c0:])
                lead = w_s[:, t0 - c0 :]
                s_ref[m, t0:, c0:] = s_ref[m, t0:, c0:] - mm_tn(lead, w_s)
                y_refs[m][t0:, :] = y_refs[m][t0:, :] - mm_tn(lead, w_y)


CHUNKS = 2
RC = 128 // CHUNKS
REL = ((1, 0), (3, 0), (2, 0), (1, 1), (3, 1), (2, 1), (0, 1))


def comm_kernel(g_ref, owners_ref, grad_ref, right_ref,
                ra, rb, sa, sb, ra2, rb2, aga, agb, pga, pgb, pbuf, prec, qbuf, qrec, part, rz, res,
                s1a, r1a, s1b, r1b, s2a, r2a, s2b, r2b, s3a, r3a, s3b, r3b,
                s4a, r4a, s4b, r4b, s5a, r5a, s5b, r5b, s6a, r6a, s6b, r6b,
                sp, rp, sza, rza, szb, rzb, local_sem, hello):
    bf = jnp.bfloat16
    me = lax.axis_index("dp")
    z = lax.axis_index("mp")
    c = me % 2
    x = (me // 2) % 4
    y = me // 8
    sent = []

    def dev(yy, xx, cc):
        return {"dp": yy * 8 + xx * 2 + cc}

    def remote(src, dst, s, r, device):
        return pltpu.make_async_remote_copy(
            src_ref=src, dst_ref=dst, send_sem=s, recv_sem=r, device_id=device, device_id_type=MESH
        )

    def send(src, dst, s, r, device):
        copy = remote(src, dst, s, r, device)
        copy.start()
        sent.append(copy)
        return copy

    own_a = pltpu.make_async_copy(g_ref.at[:, x, c, pl.ds(0, 128), :], ra.at[7], local_sem.at[0])
    own_b = pltpu.make_async_copy(g_ref.at[y, :, c, pl.ds(128, 128), :], rb.at[7], local_sem.at[1])
    own_a.start()
    own_b.start()

    barrier = pltpu.get_barrier_semaphore()
    peers = [(dev(y, (x + d) % 4, (c + e) % 2), dev((y + d) % 4, x, (c + e) % 2)) for d, e in REL]
    for pa, pb in peers:
        pl.semaphore_signal(barrier, inc=1, device_id=pa, device_id_type=MESH)
        pl.semaphore_signal(barrier, inc=1, device_id=pb, device_id_type=MESH)
    for d in (1, 7):
        pl.semaphore_signal(barrier, inc=1, device_id={"mp": (z + d) % 8}, device_id_type=MESH)
    pl.semaphore_wait(barrier, 16)

    first = [[], []]
    for k in range(CHUNKS):
        for i, (d, e) in enumerate(REL):
            xx, yy, cc = (x + d) % 4, (y + d) % 4, (c + e) % 2
            rows = pl.ds(RC * k, RC)
            first[0].append(send(g_ref.at[:, xx, cc, pl.ds(RC * k, RC), :], ra.at[i, :, rows, :],
                                 s1a.at[k, i], r1a.at[k, i], peers[i][0]))
            first[1].append(send(g_ref.at[yy, :, cc, pl.ds(128 + RC * k, RC), :], rb.at[i, :, rows, :],
                                 s1b.at[k, i], r1b.at[k, i], peers[i][1]))

    for step, span in enumerate((1, 2)):
        for d in (span, 8 - span):
            pl.semaphore_signal(hello.at[step], inc=1, device_id={"mp": (z + d) % 8}, device_id_type=MESH)
        pl.semaphore_wait(hello.at[step], 2)

    def slots_of(owner):
        seen = jnp.int32(0)
        unit = [jnp.int32(0), jnp.int32(0)]
        found = [jnp.int32(0), jnp.int32(0)]
        for u in range(32):
            hit = jnp.where(owners_ref[u] == owner, 1, 0)
            for t in range(2):
                now = jnp.where(seen == t, hit, 0)
                unit[t] = unit[t] + now * u
                found[t] = found[t] + now
            seen = seen + hit
        return unit, found

    mine, mine_found = slots_of(me)
    other, other_found = slots_of(me + 1 - 2 * c)

    def total(buf, k, at):
        acc = buf[7, at, RC * k : RC * k + RC, :].astype(F32)
        for s in range(7):
            acc = acc + buf[s, at, RC * k : RC * k + RC, :].astype(F32)
        return acc

    own_a.wait()
    own_b.wait()
    second = []
    keep = []
    for k in range(CHUNKS):
        for side in range(2):
            for i in range(7):
                first[side][7 * k + i].wait_recv()
            buf, out, land = (ra, sa, ra2) if side == 0 else (rb, sb, rb2)
            ss, rs = (s2a, r2a) if side == 0 else (s2b, r2b)
            copies = []
            for i, d in enumerate((1, 3, 2)):
                at = (y + d) % 4 if side == 0 else (x + d) % 4
                out[k, i] = total(buf, k, at)
                target = dev(at, x, c) if side == 0 else dev(y, at, c)
                copies.append(send(out.at[k, i], land.at[k, i], ss.at[k, i], rs.at[k, i], target))
            second.append(copies)
            keep.append(total(buf, k, y if side == 0 else x))
    done = []
    for k in range(CHUNKS):
        for side in range(2):
            land, gather = (ra2, aga) if side == 0 else (rb2, agb)
            ss, rs = (s3a, r3a) if side == 0 else (s3b, r3b)
            value = keep[2 * k + side]
            for i, copy in enumerate(second[2 * k + side]):
                copy.wait_recv()
                value = value + land[k, i]
            value = value.astype(bf)
            gather[k, y, x] = value
            done.append(value)
            for i, d in enumerate((1, 3, 2)):
                target = dev((y + d) % 4, x, c) if side == 0 else dev(y, (x + d) % 4, c)
                send(gather.at[k, y, x], gather.at[k, y, x], ss.at[k, i], rs.at[k, i], target)
    unit = jnp.concatenate([done[2 * k] for k in range(CHUNKS)] + [done[2 * k + 1] for k in range(CHUNKS)], axis=0)
    u0, u1 = unit[:, 0:128], unit[:, 128:256]
    for i, (p, q) in enumerate(((u0, u0), (u0, u1), (u1, u1))):
        part[i] = lax.dot_general(p, q, (((0,), (0,)), ((), ())), preferred_element_type=F32)
    zsend = []
    for j in range(7):
        zk = (z + j + 1) % 8
        zsend.append(send(part.at[:, pl.ds(pl.multiple_of(zk * 16, 16), 16), :], rz.at[j],
                          sza.at[j], rza.at[j], {"mp": zk}))
    for k in range(CHUNKS):
        for side in range(2):
            gather = aga if side == 0 else agb
            ss, rs = (s3a, r3a) if side == 0 else (s3b, r3b)
            s4, r4 = (s4a, r4a) if side == 0 else (s4b, r4b)
            for i, d in enumerate((1, 3, 2)):
                src = gather.at[k, (y + 4 - d) % 4, x] if side == 0 else gather.at[k, y, (x + 4 - d) % 4]
                target = dev((y + d) % 4, x, c) if side == 0 else dev(y, (x + d) % 4, c)
                remote(gather.at[k, y, x], src, ss.at[k, i], rs.at[k, i], target).wait_recv()
            for i, d in enumerate((1, 3, 2)):
                ref = gather.at[k, :, x] if side == 0 else gather.at[k, y]
                target = dev(y, (x + d) % 4, c) if side == 0 else dev((y + d) % 4, x, c)
                send(ref, ref, s4.at[k, i], r4.at[k, i], target)
    acc = part[:, pl.ds(pl.multiple_of(z * 16, 16), 16), :]
    for j in range(7):
        zsend[j].wait_recv()
        acc = acc + rz[j]
    pga[y, x] = acc[:, 0:8]
    pgb[y, x] = acc[:, 8:16]
    for i, d in enumerate((1, 3, 2)):
        send(pga.at[y, x], pga.at[y, x], s5a.at[i], r5a.at[i], dev((y + d) % 4, x, c))
        send(pgb.at[y, x], pgb.at[y, x], s5b.at[i], r5b.at[i], dev(y, (x + d) % 4, c))
    for i, d in enumerate((1, 3, 2)):
        remote(pga.at[y, x], pga.at[(y + 4 - d) % 4, x], s5a.at[i], r5a.at[i], dev((y + d) % 4, x, c)).wait_recv()
    for i, d in enumerate((1, 3, 2)):
        send(pga.at[:, x], pga.at[:, x], s6a.at[i], r6a.at[i], dev(y, (x + d) % 4, c))
    for i, d in enumerate((1, 3, 2)):
        remote(pgb.at[y, x], pgb.at[y, (x + 4 - d) % 4], s5b.at[i], r5b.at[i], dev(y, (x + d) % 4, c)).wait_recv()
    for i, d in enumerate((1, 3, 2)):
        send(pgb.at[y], pgb.at[y], s6b.at[i], r6b.at[i], dev((y + d) % 4, x, c))
    for k in range(CHUNKS):
        for i, d in enumerate((1, 3, 2)):
            remote(aga.at[k, :, x], aga.at[k, :, (x + 4 - d) % 4], s4a.at[k, i], r4a.at[k, i],
                   dev(y, (x + d) % 4, c)).wait_recv()
            remote(agb.at[k, y], agb.at[k, (y + 4 - d) % 4], s4b.at[k, i], r4b.at[k, i],
                   dev((y + d) % 4, x, c)).wait_recv()

    def flag_of(unit, found):
        return jnp.where(unit % 2 == c, found, 0).astype(F32)

    def pick(unit, flag):
        parts = [aga[k, unit // 8, (unit // 2) % 4] for k in range(CHUNKS)]
        parts += [agb[k, unit // 8, (unit // 2) % 4] for k in range(CHUNKS)]
        return jnp.concatenate(parts, axis=0).astype(F32) * flag

    def pick_right(unit, flag):
        at = (unit // 8, (unit // 2) % 4)
        return jnp.concatenate([pga[at[0], at[1]], pgb[at[0], at[1]]], axis=1) * flag

    for t in range(2):
        pbuf[t] = pick(other[t], flag_of(other[t], other_found[t])).astype(bf)
    pair = send(pbuf, prec, sp.at[0], rp.at[0], dev(y, x, 1 - c))
    for i, d in enumerate((1, 3, 2)):
        remote(pga.at[:, x], pga.at[:, (x + 4 - d) % 4], s6a.at[i], r6a.at[i], dev(y, (x + d) % 4, c)).wait_recv()
        remote(pgb.at[y], pgb.at[(y + 4 - d) % 4], s6b.at[i], r6b.at[i], dev((y + d) % 4, x, c)).wait_recv()
    for t in range(2):
        qbuf[t] = pick_right(other[t], flag_of(other[t], other_found[t]))
    pair_right = send(qbuf, qrec, sp.at[1], rp.at[1], dev(y, x, 1 - c))
    flags = [flag_of(mine[t], mine_found[t]) for t in range(2)]
    mine_right = [pick_right(mine[t], flags[t]) for t in range(2)]
    pair_right.wait_recv()
    for t in range(2):
        res[z, t] = mine_right[t] + qrec[t]
    zgather = []
    for j in range(7):
        send(res.at[z], res.at[z], szb.at[j], rzb.at[j], {"mp": (z + j + 1) % 8})
    pair.wait_recv()
    for t in range(2):
        grad_ref[t] = (pick(mine[t], flags[t]) + prec[t].astype(F32)).astype(bf)
    for j in range(7):
        remote(res.at[z], res.at[(z + 7 - j) % 8], szb.at[j], rzb.at[j],
               {"mp": (z + j + 1) % 8}).wait_recv()
    for k in range(8):
        for t in range(2):
            right_ref[3 * t : 3 * t + 3, 16 * k : 16 * k + 16, :] = res[k, t]
    for copy in sent:
        copy.wait_send()


def exchange(gradients, owners):
    bf, f32 = jnp.bfloat16, F32
    dma = pltpu.SemaphoreType.DMA
    ck = CHUNKS
    return pl.pallas_call(
        comm_kernel,
        out_shape=(
            jax.ShapeDtypeStruct((2, 256, 256), bf),
            jax.ShapeDtypeStruct((6, 128, 128), f32),
        ),
        in_specs=[
            pl.BlockSpec(memory_space=pl.ANY),
            pl.BlockSpec(memory_space=pltpu.SMEM),
        ],
        out_specs=(
            pl.BlockSpec(memory_space=pltpu.VMEM),
            pl.BlockSpec(memory_space=pltpu.VMEM),
        ),
        scratch_shapes=[
            pltpu.VMEM((8, 4, 128, 256), bf), pltpu.VMEM((8, 4, 128, 256), bf),
            pltpu.VMEM((ck, 3, RC, 256), f32), pltpu.VMEM((ck, 3, RC, 256), f32),
            pltpu.VMEM((ck, 3, RC, 256), f32), pltpu.VMEM((ck, 3, RC, 256), f32),
            pltpu.VMEM((ck, 4, 4, RC, 256), bf), pltpu.VMEM((ck, 4, 4, RC, 256), bf),
            pltpu.VMEM((4, 4, 3, 8, 128), f32), pltpu.VMEM((4, 4, 3, 8, 128), f32),
            pltpu.VMEM((2, 256, 256), bf), pltpu.VMEM((2, 256, 256), bf),
            pltpu.VMEM((2, 3, 16, 128), f32), pltpu.VMEM((2, 3, 16, 128), f32),
            pltpu.VMEM((3, 128, 128), f32), pltpu.VMEM((7, 3, 16, 128), f32),
            pltpu.VMEM((8, 2, 3, 16, 128), f32),
            dma((ck, 7)), dma((ck, 7)), dma((ck, 7)), dma((ck, 7)),
            dma((ck, 3)), dma((ck, 3)), dma((ck, 3)), dma((ck, 3)),
            dma((ck, 3)), dma((ck, 3)), dma((ck, 3)), dma((ck, 3)),
            dma((ck, 3)), dma((ck, 3)), dma((ck, 3)), dma((ck, 3)),
            dma((3,)), dma((3,)), dma((3,)), dma((3,)),
            dma((3,)), dma((3,)), dma((3,)), dma((3,)),
            dma((2,)), dma((2,)), dma((7,)), dma((7,)), dma((7,)), dma((7,)), dma((2,)),
            pltpu.SemaphoreType.REGULAR((2,)),
        ],
        compiler_params=pltpu.CompilerParams(collective_id=0, has_side_effects=True),
        name="exchange",
    )(gradients.reshape(4, 4, 2, 256, 256), owners)


def local_kernel(grad_ref, right_ref, l_ref, p_ref, r_ref, q_ref, m_ref, v_ref,
                 nl_ref, nlb_ref, nr_ref, nrb_ref, nm_ref, nv_ref, up_ref, work, s_ref, tg, tm):
    for t in range(2):
        g = grad_ref[t]
        new_left = 0.95 * l_ref[t] + 0.05 * lax.dot_general(
            g, g, (((1,), (1,)), ((), ())), preferred_element_type=F32
        )
        nl_ref[t] = new_left
        work[t] = mm(p_ref[t], new_left)
        s01 = right_ref[3 * t + 1]
        right_sum = jnp.concatenate(
            [
                jnp.concatenate([right_ref[3 * t], s01], axis=1),
                jnp.concatenate([s01.T, right_ref[3 * t + 2]], axis=1),
            ],
            axis=0,
        )
        new_right = 0.95 * r_ref[t] + 0.05 * right_sum
        nr_ref[t] = new_right
        work[2 + t] = mm(q_ref[t], new_right)

    def fill(t, step):
        if step == 0:
            nm_ref[t] = 0.9 * m_ref[t] + 0.1 * grad_ref[t].astype(F32)
            tg[t] = mm(p_ref[t], grad_ref[t].astype(F32))
        elif step == 1:
            tm[t] = mm(p_ref[t], nm_ref[t])
        elif step == 2:
            rot_g = mm_nt(tg[t], q_ref[t])
            nv_ref[t] = 0.95 * v_ref[t] + 0.05 * rot_g * rot_g
        elif step == 3:
            tg[t] = mm_nt(tm[t], q_ref[t]) / (jnp.sqrt(nv_ref[t]) + 1e-8)
        elif step == 4:
            tm[t] = mm_tn(p_ref[t], tg[t])
        else:
            up_ref[t] = mm(tm[t], q_ref[t])

    fillers = [functools.partial(fill, t, step) for step in range(6) for t in range(2)]
    outs = [nlb_ref.at[0], nlb_ref.at[1], nrb_ref.at[0], nrb_ref.at[1]]
    orth_all([work.at[m] for m in range(4)], s_ref, outs, fillers)


def local_step(*args):
    shape = jax.ShapeDtypeStruct((2, N, N), F32)
    vmem = pl.BlockSpec(memory_space=pltpu.VMEM)
    return pl.pallas_call(
        local_kernel,
        out_shape=(shape,) * 7,
        in_specs=[vmem] * 8,
        out_specs=(vmem,) * 7,
        scratch_shapes=[pltpu.VMEM((4, N, N), F32), pltpu.VMEM((4, N, N), F32),
                        pltpu.VMEM((2, N, N), F32), pltpu.VMEM((2, N, N), F32)],
        name="local_step",
    )(*args)


def on_device(
    gradients, owners, left_stat, left_basis, right_stat, right_basis, momentum, second_moment
):
    gradient, right_sum = exchange(gradients[0], owners)
    return local_step(
        gradient, right_sum, left_stat, left_basis, right_stat, right_basis, momentum, second_moment
    )


def solution(mesh):
    big, small = P("dp", "mp", None), P("dp", None, None)
    return jax.shard_map(
        on_device,
        mesh=mesh,
        in_specs=(P("dp", None, "mp", None), P(), big, big, small, small, big, big),
        out_specs=(big, big, small, small, big, big, big),
        check_vma=False,
    )
```

```python
import functools
import jax
import jax.numpy as jnp
from jax import lax
from jax.experimental import pallas as pl
from jax.experimental.pallas import tpu as pltpu
from jax.sharding import PartitionSpec as P

HI = lax.Precision.HIGHEST
F32 = jnp.float32
MESH = pl.DeviceIdType.MESH
NB = 64
N = 256
FILL_EVERY = 1
FILL_AT = 0


def mm(a, b):
    return lax.dot_general(a, b, (((1,), (0,)), ((), ())), precision=HI, preferred_element_type=F32)


def mm_nt(a, b):
    return lax.dot_general(a, b, (((1,), (1,)), ((), ())), precision=HI, preferred_element_type=F32)


def mm_tn(a, b):
    return lax.dot_general(a, b, (((0,), (0,)), ((), ())), precision=HI, preferred_element_type=F32)


def factor_blocks(block, fillers):
    count = block.shape[0]
    wide = 2 * NB
    sub = lax.broadcasted_iota(jnp.int32, (count, 8, wide), 1)
    done = []
    rest = block
    for q in range(NB // 8):
        if fillers:
            fillers.pop(0)()
        rows = NB - 8 * q
        cols = [
            jnp.broadcast_to(rest[:, :, 8 * q + s : 8 * q + s + 1], (count, rows, wide)) for s in range(8)
        ]
        top, rest = rest[:, 0:8, :], rest[:, 8:, :]
        scale = None
        for s in range(8):
            d = jnp.broadcast_to(cols[s][:, s : s + 1, :], (count, 8, wide))
            inv = 1.0 / d
            root = lax.rsqrt(d)
            scale = root if s == 0 else jnp.where(sub >= s, root, scale)
            mult = cols[s] * inv[:, 0:1, :]
            for s2 in range(s + 1, 8):
                cols[s2] = cols[s2] - mult * cols[s][:, s2 : s2 + 1, :]
            u = top[:, s : s + 1, :]
            if s < 7:
                top = top - jnp.where(sub > s, mult[:, 0:8, :], 0.0) * u
            if rows > 8:
                rest = rest - mult[:, 8:, :] * u
        done.append(top * scale)
    return jnp.concatenate(done, axis=1)


def orth_block(k, y_ref, s_ref, out_ref, fillers):
    count = y_ref.shape[0]
    r_i = lax.broadcasted_iota(jnp.int32, (count, NB, NB), 1)
    c_i = lax.broadcasted_iota(jnp.int32, (count, NB, NB), 2)
    k0 = k * NB
    block = jnp.concatenate([s_ref[:, k0 : k0 + NB, k0 : k0 + NB], (r_i == c_i).astype(F32)], axis=2)
    factors = factor_blocks(block, fillers)
    for m in range(count):
        inv = factors[m, :, NB : 2 * NB]
        w_y = mm(inv, y_ref[m, k0 : k0 + NB, :])
        out_ref[m, k0 : k0 + NB, :] = w_y
        t0 = k0 + NB
        if t0 < N:
            c0 = t0 // 128 * 128
            w_s = mm(inv, s_ref[m, k0 : k0 + NB, c0:])
            lead = w_s[:, t0 - c0 :]
            s_ref[m, t0:, c0:] = s_ref[m, t0:, c0:] - mm_tn(lead, w_s)
            y_ref[m, t0:, :] = y_ref[m, t0:, :] - mm_tn(lead, w_y)


def gram(y_ref, s_ref):
    for m in range(y_ref.shape[0]):
        y = y_ref[m]
        s_ref[m] = mm_nt(y, y)

CHUNKS = 2
RC = 128 // CHUNKS
REL = ((1, 0), (3, 0), (2, 0), (1, 1), (3, 1), (2, 1), (0, 1))


def comm_kernel(g_ref, owners_ref, left_in, basis_in, grad_ref, right_ref, left_ref, left_basis_ref,
                ra, rb, sa, sb, ra2, rb2, aga, agb, pga, pgb, pbuf, prec, qbuf, qrec, part, rz, res,
                s1a, r1a, s1b, r1b, s2a, r2a, s2b, r2b, s3a, r3a, s3b, r3b,
                s4a, r4a, s4b, r4b, s5a, r5a, s5b, r5b, s6a, r6a, s6b, r6b,
                sp, rp, sza, rza, szb, rzb, local_sem, hello, l_buf, p_buf, work, s_ref):
    bf = jnp.bfloat16
    me = lax.axis_index("dp")
    z = lax.axis_index("mp")
    c = me % 2
    x = (me // 2) % 4
    y = me // 8
    sent = []

    def dev(yy, xx, cc):
        return {"dp": yy * 8 + xx * 2 + cc}

    def remote(src, dst, s, r, device):
        return pltpu.make_async_remote_copy(
            src_ref=src, dst_ref=dst, send_sem=s, recv_sem=r, device_id=device, device_id_type=MESH
        )

    def send(src, dst, s, r, device):
        copy = remote(src, dst, s, r, device)
        copy.start()
        sent.append(copy)
        return copy

    own_a = pltpu.make_async_copy(g_ref.at[:, x, c, pl.ds(0, 128), :], ra.at[7], local_sem.at[0])
    own_b = pltpu.make_async_copy(g_ref.at[y, :, c, pl.ds(128, 128), :], rb.at[7], local_sem.at[1])
    own_a.start()
    own_b.start()
    load_l = pltpu.make_async_copy(left_in, l_buf, local_sem.at[2])
    load_p = pltpu.make_async_copy(basis_in, p_buf, local_sem.at[3])
    load_l.start()
    load_p.start()

    barrier = pltpu.get_barrier_semaphore()
    peers = [(dev(y, (x + d) % 4, (c + e) % 2), dev((y + d) % 4, x, (c + e) % 2)) for d, e in REL]
    for pa, pb in peers:
        pl.semaphore_signal(barrier, inc=1, device_id=pa, device_id_type=MESH)
        pl.semaphore_signal(barrier, inc=1, device_id=pb, device_id_type=MESH)
    for d in (1, 7):
        pl.semaphore_signal(barrier, inc=1, device_id={"mp": (z + d) % 8}, device_id_type=MESH)
    pl.semaphore_wait(barrier, 16)

    first = [[], []]
    for k in range(CHUNKS):
        for i, (d, e) in enumerate(REL):
            xx, yy, cc = (x + d) % 4, (y + d) % 4, (c + e) % 2
            rows = pl.ds(RC * k, RC)
            first[0].append(send(g_ref.at[:, xx, cc, pl.ds(RC * k, RC), :], ra.at[i, :, rows, :],
                                 s1a.at[k, i], r1a.at[k, i], peers[i][0]))
            first[1].append(send(g_ref.at[yy, :, cc, pl.ds(128 + RC * k, RC), :], rb.at[i, :, rows, :],
                                 s1b.at[k, i], r1b.at[k, i], peers[i][1]))

    for step, span in enumerate((1, 2)):
        for d in (span, 8 - span):
            pl.semaphore_signal(hello.at[step], inc=1, device_id={"mp": (z + d) % 8}, device_id_type=MESH)
        pl.semaphore_wait(hello.at[step], 2)

    def slots_of(owner):
        seen = jnp.int32(0)
        unit = [jnp.int32(0), jnp.int32(0)]
        found = [jnp.int32(0), jnp.int32(0)]
        for u in range(32):
            hit = jnp.where(owners_ref[u] == owner, 1, 0)
            for t in range(2):
                now = jnp.where(seen == t, hit, 0)
                unit[t] = unit[t] + now * u
                found[t] = found[t] + now
            seen = seen + hit
        return unit, found

    mine, mine_found = slots_of(me)
    other, other_found = slots_of(me + 1 - 2 * c)

    def total(buf, k, at):
        acc = buf[7, at, RC * k : RC * k + RC, :].astype(F32)
        for s in range(7):
            acc = acc + buf[s, at, RC * k : RC * k + RC, :].astype(F32)
        return acc

    own_a.wait()
    own_b.wait()
    load_l.wait()
    load_p.wait()
    second = []
    keep = []
    for k in range(CHUNKS):
        for side in range(2):
            for i in range(7):
                first[side][7 * k + i].wait_recv()
            buf, out, land = (ra, sa, ra2) if side == 0 else (rb, sb, rb2)
            ss, rs = (s2a, r2a) if side == 0 else (s2b, r2b)
            copies = []
            for i, d in enumerate((1, 3, 2)):
                at = (y + d) % 4 if side == 0 else (x + d) % 4
                out[k, i] = total(buf, k, at)
                target = dev(at, x, c) if side == 0 else dev(y, at, c)
                copies.append(send(out.at[k, i], land.at[k, i], ss.at[k, i], rs.at[k, i], target))
            second.append(copies)
            keep.append(total(buf, k, y if side == 0 else x))
    done = []
    for k in range(CHUNKS):
        for side in range(2):
            land, gather = (ra2, aga) if side == 0 else (rb2, agb)
            ss, rs = (s3a, r3a) if side == 0 else (s3b, r3b)
            value = keep[2 * k + side]
            for i, copy in enumerate(second[2 * k + side]):
                copy.wait_recv()
                value = value + land[k, i]
            value = value.astype(bf)
            gather[k, y, x] = value
            done.append(value)
            for i, d in enumerate((1, 3, 2)):
                target = dev((y + d) % 4, x, c) if side == 0 else dev(y, (x + d) % 4, c)
                send(gather.at[k, y, x], gather.at[k, y, x], ss.at[k, i], rs.at[k, i], target)
    unit = jnp.concatenate([done[2 * k] for k in range(CHUNKS)] + [done[2 * k + 1] for k in range(CHUNKS)], axis=0)
    u0, u1 = unit[:, 0:128], unit[:, 128:256]
    for i, (p, q) in enumerate(((u0, u0), (u0, u1), (u1, u1))):
        part[i] = lax.dot_general(p, q, (((0,), (0,)), ((), ())), preferred_element_type=F32)
    zsend = []
    for j in range(7):
        zk = (z + j + 1) % 8
        zsend.append(send(part.at[:, pl.ds(pl.multiple_of(zk * 16, 16), 16), :], rz.at[j],
                          sza.at[j], rza.at[j], {"mp": zk}))
    for k in range(CHUNKS):
        for side in range(2):
            gather = aga if side == 0 else agb
            ss, rs = (s3a, r3a) if side == 0 else (s3b, r3b)
            s4, r4 = (s4a, r4a) if side == 0 else (s4b, r4b)
            for i, d in enumerate((1, 3, 2)):
                src = gather.at[k, (y + 4 - d) % 4, x] if side == 0 else gather.at[k, y, (x + 4 - d) % 4]
                target = dev((y + d) % 4, x, c) if side == 0 else dev(y, (x + d) % 4, c)
                remote(gather.at[k, y, x], src, ss.at[k, i], rs.at[k, i], target).wait_recv()
            for i, d in enumerate((1, 3, 2)):
                ref = gather.at[k, :, x] if side == 0 else gather.at[k, y]
                target = dev(y, (x + d) % 4, c) if side == 0 else dev((y + d) % 4, x, c)
                send(ref, ref, s4.at[k, i], r4.at[k, i], target)
    acc = part[:, pl.ds(pl.multiple_of(z * 16, 16), 16), :]
    for j in range(7):
        zsend[j].wait_recv()
        acc = acc + rz[j]
    pga[y, x] = acc[:, 0:8]
    pgb[y, x] = acc[:, 8:16]
    for i, d in enumerate((1, 3, 2)):
        send(pga.at[y, x], pga.at[y, x], s5a.at[i], r5a.at[i], dev((y + d) % 4, x, c))
        send(pgb.at[y, x], pgb.at[y, x], s5b.at[i], r5b.at[i], dev(y, (x + d) % 4, c))
    for i, d in enumerate((1, 3, 2)):
        remote(pga.at[y, x], pga.at[(y + 4 - d) % 4, x], s5a.at[i], r5a.at[i], dev((y + d) % 4, x, c)).wait_recv()
    for i, d in enumerate((1, 3, 2)):
        send(pga.at[:, x], pga.at[:, x], s6a.at[i], r6a.at[i], dev(y, (x + d) % 4, c))
    for i, d in enumerate((1, 3, 2)):
        remote(pgb.at[y, x], pgb.at[y, (x + 4 - d) % 4], s5b.at[i], r5b.at[i], dev(y, (x + d) % 4, c)).wait_recv()
    for i, d in enumerate((1, 3, 2)):
        send(pgb.at[y], pgb.at[y], s6b.at[i], r6b.at[i], dev((y + d) % 4, x, c))
    for k in range(CHUNKS):
        for i, d in enumerate((1, 3, 2)):
            remote(aga.at[k, :, x], aga.at[k, :, (x + 4 - d) % 4], s4a.at[k, i], r4a.at[k, i],
                   dev(y, (x + d) % 4, c)).wait_recv()
            remote(agb.at[k, y], agb.at[k, (y + 4 - d) % 4], s4b.at[k, i], r4b.at[k, i],
                   dev((y + d) % 4, x, c)).wait_recv()

    def flag_of(unit, found):
        return jnp.where(unit % 2 == c, found, 0).astype(F32)

    def pick(unit, flag):
        parts = [aga[k, unit // 8, (unit // 2) % 4] for k in range(CHUNKS)]
        parts += [agb[k, unit // 8, (unit // 2) % 4] for k in range(CHUNKS)]
        return jnp.concatenate(parts, axis=0).astype(F32) * flag

    def pick_right(unit, flag):
        at = (unit // 8, (unit // 2) % 4)
        return jnp.concatenate([pga[at[0], at[1]], pgb[at[0], at[1]]], axis=1) * flag

    for t in range(2):
        pbuf[t] = pick(other[t], flag_of(other[t], other_found[t])).astype(bf)
    pair = send(pbuf, prec, sp.at[0], rp.at[0], dev(y, x, 1 - c))
    flags = [flag_of(mine[t], mine_found[t]) for t in range(2)]
    kept = [pick(mine[t], flags[t]) for t in range(2)]
    pair.wait_recv()
    for t in range(2):
        grad = (kept[t] + prec[t].astype(F32)).astype(bf)
        grad_ref[t] = grad
        new_left = 0.95 * l_buf[t] + 0.05 * lax.dot_general(
            grad, grad, (((1,), (1,)), ((), ())), preferred_element_type=F32
        )
        left_ref[t] = new_left
        work[t] = mm(p_buf[t], new_left)
    for i, d in enumerate((1, 3, 2)):
        remote(pga.at[:, x], pga.at[:, (x + 4 - d) % 4], s6a.at[i], r6a.at[i], dev(y, (x + d) % 4, c)).wait_recv()
        remote(pgb.at[y], pgb.at[(y + 4 - d) % 4], s6b.at[i], r6b.at[i], dev((y + d) % 4, x, c)).wait_recv()
    for t in range(2):
        qbuf[t] = pick_right(other[t], flag_of(other[t], other_found[t]))
    pair_right = send(qbuf, qrec, sp.at[1], rp.at[1], dev(y, x, 1 - c))
    mine_right = [pick_right(mine[t], flags[t]) for t in range(2)]
    gram(work, s_ref)
    pair_right.wait_recv()
    for t in range(2):
        res[z, t] = mine_right[t] + qrec[t]
    for j in range(7):
        send(res.at[z], res.at[z], szb.at[j], rzb.at[j], {"mp": (z + j + 1) % 8})
    for k in range(N // NB):
        orth_block(k, work, s_ref, left_basis_ref, [])
    for j in range(7):
        remote(res.at[z], res.at[(z + 7 - j) % 8], szb.at[j], rzb.at[j],
               {"mp": (z + j + 1) % 8}).wait_recv()
    for k in range(8):
        for t in range(2):
            right_ref[3 * t : 3 * t + 3, 16 * k : 16 * k + 16, :] = res[k, t]
    for copy in sent:
        copy.wait_send()


def exchange(gradients, owners, left_stat, left_basis):
    bf, f32 = jnp.bfloat16, F32
    dma = pltpu.SemaphoreType.DMA
    ck = CHUNKS
    return pl.pallas_call(
        comm_kernel,
        out_shape=(
            jax.ShapeDtypeStruct((2, 256, 256), bf),
            jax.ShapeDtypeStruct((6, 128, 128), f32),
            jax.ShapeDtypeStruct((2, N, N), f32),
            jax.ShapeDtypeStruct((2, N, N), f32),
        ),
        in_specs=[
            pl.BlockSpec(memory_space=pl.ANY),
            pl.BlockSpec(memory_space=pltpu.SMEM),
            pl.BlockSpec(memory_space=pl.ANY),
            pl.BlockSpec(memory_space=pl.ANY),
        ],
        out_specs=(pl.BlockSpec(memory_space=pltpu.VMEM),) * 4,
        scratch_shapes=[
            pltpu.VMEM((8, 4, 128, 256), bf), pltpu.VMEM((8, 4, 128, 256), bf),
            pltpu.VMEM((ck, 3, RC, 256), f32), pltpu.VMEM((ck, 3, RC, 256), f32),
            pltpu.VMEM((ck, 3, RC, 256), f32), pltpu.VMEM((ck, 3, RC, 256), f32),
            pltpu.VMEM((ck, 4, 4, RC, 256), bf), pltpu.VMEM((ck, 4, 4, RC, 256), bf),
            pltpu.VMEM((4, 4, 3, 8, 128), f32), pltpu.VMEM((4, 4, 3, 8, 128), f32),
            pltpu.VMEM((2, 256, 256), bf), pltpu.VMEM((2, 256, 256), bf),
            pltpu.VMEM((2, 3, 16, 128), f32), pltpu.VMEM((2, 3, 16, 128), f32),
            pltpu.VMEM((3, 128, 128), f32), pltpu.VMEM((7, 3, 16, 128), f32),
            pltpu.VMEM((8, 2, 3, 16, 128), f32),
            dma((ck, 7)), dma((ck, 7)), dma((ck, 7)), dma((ck, 7)),
            dma((ck, 3)), dma((ck, 3)), dma((ck, 3)), dma((ck, 3)),
            dma((ck, 3)), dma((ck, 3)), dma((ck, 3)), dma((ck, 3)),
            dma((ck, 3)), dma((ck, 3)), dma((ck, 3)), dma((ck, 3)),
            dma((3,)), dma((3,)), dma((3,)), dma((3,)),
            dma((3,)), dma((3,)), dma((3,)), dma((3,)),
            dma((2,)), dma((2,)), dma((7,)), dma((7,)), dma((7,)), dma((7,)), dma((4,)),
            pltpu.SemaphoreType.REGULAR((2,)),
            pltpu.VMEM((2, N, N), f32), pltpu.VMEM((2, N, N), f32),
            pltpu.VMEM((2, N, N), f32), pltpu.VMEM((2, N, N), f32),
        ],
        compiler_params=pltpu.CompilerParams(collective_id=0, has_side_effects=True),
        name="exchange",
    )(gradients.reshape(4, 4, 2, 256, 256), owners, left_stat, left_basis)


def local_kernel(grad_ref, right_ref, left_ref, left_basis_ref, p_ref, r_ref, q_ref, m_ref, v_ref,
                 nl_ref, nlb_ref, nr_ref, nrb_ref, nm_ref, nv_ref, up_ref, work, s_ref, tg, tm):
    for t in range(2):
        s01 = right_ref[3 * t + 1]
        right_sum = jnp.concatenate(
            [
                jnp.concatenate([right_ref[3 * t], s01], axis=1),
                jnp.concatenate([s01.T, right_ref[3 * t + 2]], axis=1),
            ],
            axis=0,
        )
        new_right = 0.95 * r_ref[t] + 0.05 * right_sum
        nr_ref[t] = new_right
        work[t] = mm(q_ref[t], new_right)
    gram(work, s_ref)

    def fill(t, step):
        if step == 0:
            nm_ref[t] = 0.9 * m_ref[t] + 0.1 * grad_ref[t].astype(F32)
            tg[t] = mm(p_ref[t], grad_ref[t].astype(F32))
        elif step == 1:
            tm[t] = mm(p_ref[t], nm_ref[t])
        elif step == 2:
            rot_g = mm_nt(tg[t], q_ref[t])
            nv_ref[t] = 0.95 * v_ref[t] + 0.05 * rot_g * rot_g
        elif step == 3:
            tg[t] = mm_nt(tm[t], q_ref[t]) / (jnp.sqrt(nv_ref[t]) + 1e-8)
        elif step == 4:
            tm[t] = mm_tn(p_ref[t], tg[t])
        elif step == 5:
            up_ref[t] = mm(tm[t], q_ref[t])
        elif step == 6:
            nl_ref[t] = left_ref[t]
        else:
            nlb_ref[t] = left_basis_ref[t]

    fillers = [functools.partial(fill, t, step) for step in range(8) for t in range(2)]
    for k in range(N // NB):
        orth_block(k, work, s_ref, nrb_ref, fillers)


def local_step(*args):
    shape = jax.ShapeDtypeStruct((2, N, N), F32)
    vmem = pl.BlockSpec(memory_space=pltpu.VMEM)
    return pl.pallas_call(
        local_kernel,
        out_shape=(shape,) * 7,
        in_specs=[vmem] * 9,
        out_specs=(vmem,) * 7,
        scratch_shapes=[pltpu.VMEM((2, N, N), F32)] * 4,
        name="local_step",
    )(*args)


def on_device(
    gradients, owners, left_stat, left_basis, right_stat, right_basis, momentum, second_moment
):
    gradient, right_sum, new_left, new_left_basis = exchange(
        gradients[0], owners, left_stat, left_basis
    )
    return local_step(
        gradient, right_sum, new_left, new_left_basis, left_basis,
        right_stat, right_basis, momentum, second_moment,
    )


def solution(mesh):
    big, small = P("dp", "mp", None), P("dp", None, None)
    return jax.shard_map(
        on_device,
        mesh=mesh,
        in_specs=(P("dp", None, "mp", None), P(), big, big, small, small, big, big),
        out_specs=(big, big, small, small, big, big, big),
        check_vma=False,
    )
```

```python
import functools
import jax
import jax.numpy as jnp
from jax import lax
from jax.experimental import pallas as pl
from jax.experimental.pallas import tpu as pltpu
from jax.sharding import PartitionSpec as P

HI = lax.Precision.HIGHEST
F32 = jnp.float32
MESH = pl.DeviceIdType.MESH
NB = 64
N = 256
FILL_EVERY = 1
FILL_AT = 0


def mm(a, b):
    return lax.dot_general(a, b, (((1,), (0,)), ((), ())), precision=HI, preferred_element_type=F32)


def mm_nt(a, b):
    return lax.dot_general(a, b, (((1,), (1,)), ((), ())), precision=HI, preferred_element_type=F32)


def mm_tn(a, b):
    return lax.dot_general(a, b, (((0,), (0,)), ((), ())), precision=HI, preferred_element_type=F32)


def factor_blocks(block, fillers):
    count = block.shape[0]
    wide = 2 * NB
    sub = lax.broadcasted_iota(jnp.int32, (count, 8, wide), 1)
    done = []
    rest = block
    for q in range(NB // 8):
        if fillers:
            fillers.pop(0)()
        rows = NB - 8 * q
        cols = [
            jnp.broadcast_to(rest[:, :, 8 * q + s : 8 * q + s + 1], (count, rows, wide)) for s in range(8)
        ]
        top, rest = rest[:, 0:8, :], rest[:, 8:, :]
        scale = None
        for s in range(8):
            d = jnp.broadcast_to(cols[s][:, s : s + 1, :], (count, 8, wide))
            inv = 1.0 / d
            root = lax.rsqrt(d)
            scale = root if s == 0 else jnp.where(sub >= s, root, scale)
            mult = cols[s] * inv[:, 0:1, :]
            for s2 in range(s + 1, 8):
                cols[s2] = cols[s2] - mult * cols[s][:, s2 : s2 + 1, :]
            u = top[:, s : s + 1, :]
            if s < 7:
                top = top - jnp.where(sub > s, mult[:, 0:8, :], 0.0) * u
            if rows > 8:
                rest = rest - mult[:, 8:, :] * u
        done.append(top * scale)
    return jnp.concatenate(done, axis=1)


def orth_block(k, y_ref, s_ref, out_ref, fillers):
    count = y_ref.shape[0]
    r_i = lax.broadcasted_iota(jnp.int32, (count, NB, NB), 1)
    c_i = lax.broadcasted_iota(jnp.int32, (count, NB, NB), 2)
    k0 = k * NB
    block = jnp.concatenate([s_ref[:, k0 : k0 + NB, k0 : k0 + NB], (r_i == c_i).astype(F32)], axis=2)
    factors = factor_blocks(block, fillers)
    for m in range(count):
        inv = factors[m, :, NB : 2 * NB]
        w_y = mm(inv, y_ref[m, k0 : k0 + NB, :])
        out_ref[m, k0 : k0 + NB, :] = w_y
        t0 = k0 + NB
        if t0 < N:
            c0 = t0 // 128 * 128
            w_s = mm(inv, s_ref[m, k0 : k0 + NB, c0:])
            lead = w_s[:, t0 - c0 :]
            s_ref[m, t0:, c0:] = s_ref[m, t0:, c0:] - mm_tn(lead, w_s)
            y_ref[m, t0:, :] = y_ref[m, t0:, :] - mm_tn(lead, w_y)


def gram(y_ref, s_ref):
    for m in range(y_ref.shape[0]):
        y = y_ref[m]
        s_ref[m] = mm_nt(y, y)

CHUNKS = 4
RC = 128 // CHUNKS
REL = ((1, 0), (3, 0), (2, 0), (1, 1), (3, 1), (2, 1), (0, 1))


def comm_kernel(g_ref, owners_ref, left_in, basis_in, moment_in, right_in, grad_ref, right_ref, left_ref, left_basis_ref, rot_ref,
                ra, rb, sa, sb, ra2, rb2, aga, agb, pga, pgb, pbuf, prec, qbuf, qrec, part, rz, res,
                s1a, r1a, s1b, r1b, s2a, r2a, s2b, r2b, s3a, r3a, s3b, r3b,
                s4a, r4a, s4b, r4b, s5a, r5a, s5b, r5b, s6a, r6a, s6b, r6b,
                sp, rp, sza, rza, szb, rzb, local_sem, hello, l_buf, p_buf, work, s_ref, m_buf, q_buf):
    bf = jnp.bfloat16
    me = lax.axis_index("dp")
    z = lax.axis_index("mp")
    c = me % 2
    x = (me // 2) % 4
    y = me // 8
    sent = []

    def dev(yy, xx, cc):
        return {"dp": yy * 8 + xx * 2 + cc}

    def remote(src, dst, s, r, device):
        return pltpu.make_async_remote_copy(
            src_ref=src, dst_ref=dst, send_sem=s, recv_sem=r, device_id=device, device_id_type=MESH
        )

    def send(src, dst, s, r, device):
        copy = remote(src, dst, s, r, device)
        copy.start()
        sent.append(copy)
        return copy

    own_a = pltpu.make_async_copy(g_ref.at[:, x, c, pl.ds(0, 128), :], ra.at[7], local_sem.at[0])
    own_b = pltpu.make_async_copy(g_ref.at[y, :, c, pl.ds(128, 128), :], rb.at[7], local_sem.at[1])
    own_a.start()
    own_b.start()
    load_l = pltpu.make_async_copy(left_in, l_buf, local_sem.at[2])
    load_p = pltpu.make_async_copy(basis_in, p_buf, local_sem.at[3])
    load_l.start()
    load_p.start()
    load_m = pltpu.make_async_copy(moment_in, m_buf, local_sem.at[4])
    load_q = pltpu.make_async_copy(right_in, q_buf, local_sem.at[5])
    load_m.start()
    load_q.start()

    barrier = pltpu.get_barrier_semaphore()
    peers = [(dev(y, (x + d) % 4, (c + e) % 2), dev((y + d) % 4, x, (c + e) % 2)) for d, e in REL]
    for pa, pb in peers:
        pl.semaphore_signal(barrier, inc=1, device_id=pa, device_id_type=MESH)
        pl.semaphore_signal(barrier, inc=1, device_id=pb, device_id_type=MESH)
    for d in (1, 7):
        pl.semaphore_signal(barrier, inc=1, device_id={"mp": (z + d) % 8}, device_id_type=MESH)
    pl.semaphore_wait(barrier, 16)

    first = [[], []]
    for k in range(CHUNKS):
        for i, (d, e) in enumerate(REL):
            xx, yy, cc = (x + d) % 4, (y + d) % 4, (c + e) % 2
            rows = pl.ds(RC * k, RC)
            first[0].append(send(g_ref.at[:, xx, cc, pl.ds(RC * k, RC), :], ra.at[i, :, rows, :],
                                 s1a.at[k, i], r1a.at[k, i], peers[i][0]))
            first[1].append(send(g_ref.at[yy, :, cc, pl.ds(128 + RC * k, RC), :], rb.at[i, :, rows, :],
                                 s1b.at[k, i], r1b.at[k, i], peers[i][1]))

    for step, span in enumerate((1, 2)):
        for d in (span, 8 - span):
            pl.semaphore_signal(hello.at[step], inc=1, device_id={"mp": (z + d) % 8}, device_id_type=MESH)
        pl.semaphore_wait(hello.at[step], 2)

    def slots_of(owner):
        seen = jnp.int32(0)
        unit = [jnp.int32(0), jnp.int32(0)]
        found = [jnp.int32(0), jnp.int32(0)]
        for u in range(32):
            hit = jnp.where(owners_ref[u] == owner, 1, 0)
            for t in range(2):
                now = jnp.where(seen == t, hit, 0)
                unit[t] = unit[t] + now * u
                found[t] = found[t] + now
            seen = seen + hit
        return unit, found

    mine, mine_found = slots_of(me)
    other, other_found = slots_of(me + 1 - 2 * c)

    def total(buf, k, at):
        acc = buf[7, at, RC * k : RC * k + RC, :].astype(F32)
        for s in range(7):
            acc = acc + buf[s, at, RC * k : RC * k + RC, :].astype(F32)
        return acc

    load_l.wait()
    load_p.wait()
    load_m.wait()
    load_q.wait()
    for t in range(2):
        rot_ref[t] = mm_nt(mm(p_buf[t], m_buf[t]), q_buf[t])
    own_a.wait()
    own_b.wait()
    second = []
    keep = []
    for k in range(CHUNKS):
        for side in range(2):
            for i in range(7):
                first[side][7 * k + i].wait_recv()
            buf, out, land = (ra, sa, ra2) if side == 0 else (rb, sb, rb2)
            ss, rs = (s2a, r2a) if side == 0 else (s2b, r2b)
            copies = []
            for i, d in enumerate((1, 3, 2)):
                at = (y + d) % 4 if side == 0 else (x + d) % 4
                out[k, i] = total(buf, k, at)
                target = dev(at, x, c) if side == 0 else dev(y, at, c)
                copies.append(send(out.at[k, i], land.at[k, i], ss.at[k, i], rs.at[k, i], target))
            second.append(copies)
            keep.append(total(buf, k, y if side == 0 else x))
    done = []
    for k in range(CHUNKS):
        for side in range(2):
            land, gather = (ra2, aga) if side == 0 else (rb2, agb)
            ss, rs = (s3a, r3a) if side == 0 else (s3b, r3b)
            value = keep[2 * k + side]
            for i, copy in enumerate(second[2 * k + side]):
                copy.wait_recv()
                value = value + land[k, i]
            value = value.astype(bf)
            gather[k, y, x] = value
            done.append(value)
            for i, d in enumerate((1, 3, 2)):
                target = dev((y + d) % 4, x, c) if side == 0 else dev(y, (x + d) % 4, c)
                send(gather.at[k, y, x], gather.at[k, y, x], ss.at[k, i], rs.at[k, i], target)
    unit = jnp.concatenate([done[2 * k] for k in range(CHUNKS)] + [done[2 * k + 1] for k in range(CHUNKS)], axis=0)
    u0, u1 = unit[:, 0:128], unit[:, 128:256]
    for i, (p, q) in enumerate(((u0, u0), (u0, u1), (u1, u1))):
        part[i] = lax.dot_general(p, q, (((0,), (0,)), ((), ())), preferred_element_type=F32)
    zsend = []
    for j in range(7):
        zk = (z + j + 1) % 8
        zsend.append(send(part.at[:, pl.ds(pl.multiple_of(zk * 16, 16), 16), :], rz.at[j],
                          sza.at[j], rza.at[j], {"mp": zk}))
    for k in range(CHUNKS):
        for side in range(2):
            gather = aga if side == 0 else agb
            ss, rs = (s3a, r3a) if side == 0 else (s3b, r3b)
            for i, d in enumerate((1, 3, 2)):
                src = gather.at[k, (y + 4 - d) % 4, x] if side == 0 else gather.at[k, y, (x + 4 - d) % 4]
                target = dev((y + d) % 4, x, c) if side == 0 else dev(y, (x + d) % 4, c)
                remote(gather.at[k, y, x], src, ss.at[k, i], rs.at[k, i], target).wait_recv()
        if k == CHUNKS - 1:
            acc = part[:, pl.ds(pl.multiple_of(z * 16, 16), 16), :]
            for j in range(7):
                zsend[j].wait_recv()
                acc = acc + rz[j]
            pga[y, x] = acc[:, 0:8]
            pgb[y, x] = acc[:, 8:16]
            for i, d in enumerate((1, 3, 2)):
                send(pga.at[y, x], pga.at[y, x], s5a.at[i], r5a.at[i], dev((y + d) % 4, x, c))
                send(pgb.at[y, x], pgb.at[y, x], s5b.at[i], r5b.at[i], dev(y, (x + d) % 4, c))
        for side in range(2):
            gather = aga if side == 0 else agb
            s4, r4 = (s4a, r4a) if side == 0 else (s4b, r4b)
            for i, d in enumerate((1, 3, 2)):
                ref = gather.at[k, :, x] if side == 0 else gather.at[k, y]
                target = dev(y, (x + d) % 4, c) if side == 0 else dev((y + d) % 4, x, c)
                send(ref, ref, s4.at[k, i], r4.at[k, i], target)
    for i, d in enumerate((1, 3, 2)):
        remote(pga.at[y, x], pga.at[(y + 4 - d) % 4, x], s5a.at[i], r5a.at[i], dev((y + d) % 4, x, c)).wait_recv()
    for i, d in enumerate((1, 3, 2)):
        send(pga.at[:, x], pga.at[:, x], s6a.at[i], r6a.at[i], dev(y, (x + d) % 4, c))
    for i, d in enumerate((1, 3, 2)):
        remote(pgb.at[y, x], pgb.at[y, (x + 4 - d) % 4], s5b.at[i], r5b.at[i], dev(y, (x + d) % 4, c)).wait_recv()
    for i, d in enumerate((1, 3, 2)):
        send(pgb.at[y], pgb.at[y], s6b.at[i], r6b.at[i], dev((y + d) % 4, x, c))
    for k in range(CHUNKS):
        for i, d in enumerate((1, 3, 2)):
            remote(aga.at[k, :, x], aga.at[k, :, (x + 4 - d) % 4], s4a.at[k, i], r4a.at[k, i],
                   dev(y, (x + d) % 4, c)).wait_recv()
            remote(agb.at[k, y], agb.at[k, (y + 4 - d) % 4], s4b.at[k, i], r4b.at[k, i],
                   dev((y + d) % 4, x, c)).wait_recv()

    def flag_of(unit, found):
        return jnp.where(unit % 2 == c, found, 0).astype(F32)

    def pick(unit, flag):
        parts = [aga[k, unit // 8, (unit // 2) % 4] for k in range(CHUNKS)]
        parts += [agb[k, unit // 8, (unit // 2) % 4] for k in range(CHUNKS)]
        return jnp.concatenate(parts, axis=0).astype(F32) * flag

    def pick_right(unit, flag):
        at = (unit // 8, (unit // 2) % 4)
        return jnp.concatenate([pga[at[0], at[1]], pgb[at[0], at[1]]], axis=1) * flag

    for t in range(2):
        pbuf[t] = pick(other[t], flag_of(other[t], other_found[t])).astype(bf)
    pair = send(pbuf, prec, sp.at[0], rp.at[0], dev(y, x, 1 - c))
    flags = [flag_of(mine[t], mine_found[t]) for t in range(2)]
    kept = [pick(mine[t], flags[t]) for t in range(2)]
    pair.wait_recv()
    for t in range(2):
        grad = (kept[t] + prec[t].astype(F32)).astype(bf)
        grad_ref[t] = grad
        new_left = 0.95 * l_buf[t] + 0.05 * lax.dot_general(
            grad, grad, (((1,), (1,)), ((), ())), preferred_element_type=F32
        )
        left_ref[t] = new_left
        work[t] = mm(p_buf[t], new_left)
    for i, d in enumerate((1, 3, 2)):
        remote(pga.at[:, x], pga.at[:, (x + 4 - d) % 4], s6a.at[i], r6a.at[i], dev(y, (x + d) % 4, c)).wait_recv()
        remote(pgb.at[y], pgb.at[(y + 4 - d) % 4], s6b.at[i], r6b.at[i], dev((y + d) % 4, x, c)).wait_recv()
    for t in range(2):
        qbuf[t] = pick_right(other[t], flag_of(other[t], other_found[t]))
    pair_right = send(qbuf, qrec, sp.at[1], rp.at[1], dev(y, x, 1 - c))
    mine_right = [pick_right(mine[t], flags[t]) for t in range(2)]
    gram(work, s_ref)
    pair_right.wait_recv()
    for t in range(2):
        res[z, t] = mine_right[t] + qrec[t]
    for j in range(7):
        send(res.at[z], res.at[z], szb.at[j], rzb.at[j], {"mp": (z + j + 1) % 8})
    for k in range(N // NB):
        orth_block(k, work, s_ref, left_basis_ref, [])
    for j in range(7):
        remote(res.at[z], res.at[(z + 7 - j) % 8], szb.at[j], rzb.at[j],
               {"mp": (z + j + 1) % 8}).wait_recv()
    for k in range(8):
        for t in range(2):
            right_ref[3 * t : 3 * t + 3, 16 * k : 16 * k + 16, :] = res[k, t]
    for copy in sent:
        copy.wait_send()


def exchange(gradients, owners, left_stat, left_basis, momentum, right_basis):
    bf, f32 = jnp.bfloat16, F32
    dma = pltpu.SemaphoreType.DMA
    ck = CHUNKS
    return pl.pallas_call(
        comm_kernel,
        out_shape=(
            jax.ShapeDtypeStruct((2, 256, 256), bf),
            jax.ShapeDtypeStruct((6, 128, 128), f32),
            jax.ShapeDtypeStruct((2, N, N), f32),
            jax.ShapeDtypeStruct((2, N, N), f32),
            jax.ShapeDtypeStruct((2, N, N), f32),
        ),
        in_specs=[
            pl.BlockSpec(memory_space=pl.ANY),
            pl.BlockSpec(memory_space=pltpu.SMEM),
            pl.BlockSpec(memory_space=pl.ANY),
            pl.BlockSpec(memory_space=pl.ANY),
            pl.BlockSpec(memory_space=pl.ANY),
            pl.BlockSpec(memory_space=pl.ANY),
        ],
        out_specs=(pl.BlockSpec(memory_space=pltpu.VMEM),) * 5,
        scratch_shapes=[
            pltpu.VMEM((8, 4, 128, 256), bf), pltpu.VMEM((8, 4, 128, 256), bf),
            pltpu.VMEM((ck, 3, RC, 256), f32), pltpu.VMEM((ck, 3, RC, 256), f32),
            pltpu.VMEM((ck, 3, RC, 256), f32), pltpu.VMEM((ck, 3, RC, 256), f32),
            pltpu.VMEM((ck, 4, 4, RC, 256), bf), pltpu.VMEM((ck, 4, 4, RC, 256), bf),
            pltpu.VMEM((4, 4, 3, 8, 128), f32), pltpu.VMEM((4, 4, 3, 8, 128), f32),
            pltpu.VMEM((2, 256, 256), bf), pltpu.VMEM((2, 256, 256), bf),
            pltpu.VMEM((2, 3, 16, 128), f32), pltpu.VMEM((2, 3, 16, 128), f32),
            pltpu.VMEM((3, 128, 128), f32), pltpu.VMEM((7, 3, 16, 128), f32),
            pltpu.VMEM((8, 2, 3, 16, 128), f32),
            dma((ck, 7)), dma((ck, 7)), dma((ck, 7)), dma((ck, 7)),
            dma((ck, 3)), dma((ck, 3)), dma((ck, 3)), dma((ck, 3)),
            dma((ck, 3)), dma((ck, 3)), dma((ck, 3)), dma((ck, 3)),
            dma((ck, 3)), dma((ck, 3)), dma((ck, 3)), dma((ck, 3)),
            dma((3,)), dma((3,)), dma((3,)), dma((3,)),
            dma((3,)), dma((3,)), dma((3,)), dma((3,)),
            dma((2,)), dma((2,)), dma((7,)), dma((7,)), dma((7,)), dma((7,)), dma((6,)),
            pltpu.SemaphoreType.REGULAR((2,)),
            pltpu.VMEM((2, N, N), f32), pltpu.VMEM((2, N, N), f32),
            pltpu.VMEM((2, N, N), f32), pltpu.VMEM((2, N, N), f32),
            pltpu.VMEM((2, N, N), f32), pltpu.VMEM((2, N, N), f32),
        ],
        compiler_params=pltpu.CompilerParams(collective_id=0, has_side_effects=True),
        name="exchange",
    )(gradients.reshape(4, 4, 2, 256, 256), owners, left_stat, left_basis, momentum, right_basis)


def local_kernel(right_ref, r_ref, q_ref, grad_in, left_in, left_basis_in, p_in, m_in, v_in, rot_in,
                 nl_out, nlb_out, nr_out, nrb_out, nm_out, nv_out, up_out,
                 work, s_ref, tg, tm, grad, p_buf, m_buf, v_buf, left, left_basis,
                 nr, nrb, up, rot, in_sem, out_sem):
    loads = {}
    for i, (name, src, dst) in enumerate((
        ("p", p_in, p_buf), ("g", grad_in, grad), ("m", m_in, m_buf), ("v", v_in, v_buf),
        ("b", rot_in, rot), ("l", left_in, left), ("lb", left_basis_in, left_basis),
    )):
        loads[name] = pltpu.make_async_copy(src, dst, in_sem.at[i])
        loads[name].start()
    stores = []

    def store(src, dst):
        copy = pltpu.make_async_copy(src, dst, out_sem.at[len(stores)])
        copy.start()
        stores.append(copy)

    for t in range(2):
        s01 = right_ref[3 * t + 1]
        right_sum = jnp.concatenate(
            [
                jnp.concatenate([right_ref[3 * t], s01], axis=1),
                jnp.concatenate([s01.T, right_ref[3 * t + 2]], axis=1),
            ],
            axis=0,
        )
        new_right = 0.95 * r_ref[t] + 0.05 * right_sum
        nr[t] = new_right
        work[t] = mm(q_ref[t], new_right)
    gram(work, s_ref)
    for name in ("p", "g", "m", "v", "b", "l", "lb"):
        loads[name].wait()
    store(left, nl_out)
    store(left_basis, nlb_out)
    store(nr, nr_out)

    def fill(t, step):
        if step == 0:
            m_buf[t] = 0.9 * m_buf[t] + 0.1 * grad[t].astype(F32)
            tg[t] = mm(p_buf[t], grad[t].astype(F32))
        elif step == 1:
            rot_g = mm_nt(tg[t], q_ref[t])
            v_buf[t] = 0.95 * v_buf[t] + 0.05 * rot_g * rot_g
            tg[t] = (0.9 * rot[t] + 0.1 * rot_g) / (jnp.sqrt(v_buf[t]) + 1e-8)
        elif step == 2:
            tm[t] = mm_tn(p_buf[t], tg[t])
        else:
            up[t] = mm(tm[t], q_ref[t])

    fillers = [functools.partial(fill, t, step) for step in range(4) for t in range(2)]
    for k in range(N // NB):
        orth_block(k, work, s_ref, nrb, fillers)
        if k == 1:
            store(m_buf, nm_out)
            store(v_buf, nv_out)
            store(up, up_out)
        store(nrb.at[:, NB * k : NB * k + NB, :], nrb_out.at[:, NB * k : NB * k + NB, :])
    for copy in stores:
        copy.wait()


def local_step(gradient, right_sum, new_left, new_left_basis, left_basis, right_stat, right_basis, momentum, second, rotated):
    shape = jax.ShapeDtypeStruct((2, N, N), F32)
    vmem = pl.BlockSpec(memory_space=pltpu.VMEM)
    anywhere = pl.BlockSpec(memory_space=pl.ANY)
    buf = pltpu.VMEM((2, N, N), F32)
    return pl.pallas_call(
        local_kernel,
        out_shape=(shape,) * 7,
        in_specs=[vmem] * 3 + [anywhere] * 7,
        out_specs=(anywhere,) * 7,
        scratch_shapes=[buf] * 4 + [pltpu.VMEM((2, N, N), jnp.bfloat16)] + [buf] * 9
        + [pltpu.SemaphoreType.DMA((7,)), pltpu.SemaphoreType.DMA((10,))],
        name="local_step",
    )(right_sum, right_stat, right_basis, gradient, new_left, new_left_basis, left_basis, momentum, second, rotated)


def on_device(
    gradients, owners, left_stat, left_basis, right_stat, right_basis, momentum, second_moment
):
    gradient, right_sum, new_left, new_left_basis, rotated = exchange(
        gradients[0], owners, left_stat, left_basis, momentum, right_basis
    )
    return local_step(
        gradient, right_sum, new_left, new_left_basis, left_basis,
        right_stat, right_basis, momentum, second_moment, rotated,
    )


def solution(mesh):
    big, small = P("dp", "mp", None), P("dp", None, None)
    return jax.shard_map(
        on_device,
        mesh=mesh,
        in_specs=(P("dp", None, "mp", None), P(), big, big, small, small, big, big),
        out_specs=(big, big, small, small, big, big, big),
        check_vma=False,
    )
```
